32 devices in a mesh: group: 4 (over y, x), ctx: 8 (over z, core).
Axes of the slice: x: 2, y: 2, z: 4, core: 2. Of those that a mesh axis runs over, the one named last changes fastest.
Arguments:
- hidden_in: bfloat16 [256, 4096], P(('group', 'ctx')), may hold values from -3 to 3
- queries: bfloat16 [256, 4096], P(('group', 'ctx')), may hold values from -120 to 120
- block_kv: bfloat16 [256, 2, 512], P(('group', 'ctx')), may hold values from -4 to 4
- cache: bfloat16 [8, 2, 4096, 512], P('group', None, 'ctx'), may hold values from -4 to 4
- lengths: int32 [8], P('group'), may hold values from 2 to 4096
- out_proj: bfloat16 [4096, 4096], P('ctx'), may hold values from -1.5 to 1.5
- norm_gain: float32 [4096], replicated, may hold values from 0.1 to 1.9
- expert_ids: int32 [256, 8], P(('group', 'ctx')), may hold values from 0 to 31, all different within a row; in each aligned block of 8 rows (0 to 7, 8 to 15, ...) at most 4 rows name the same one
- gate_weights: float32 [256, 8], P(('group', 'ctx')), may hold values from 0.05 to 1
- expert_gate: bfloat16 [32, 4096, 512], P(('group', 'ctx')), may hold values from -0.09375 to 0.09375
- expert_up: bfloat16 [32, 4096, 512], P(('group', 'ctx')), may hold values from -0.09375 to 0.09375
- expert_down: bfloat16 [32, 512, 4096], P(('group', 'ctx')), may hold values from -0.25 to 0.25
Outputs:
- attended: bfloat16 [256, 4096], P(('group', 'ctx'))
- layer_out: bfloat16 [256, 4096], P(('group', 'ctx'))
The draws below stay inside these ranges and needn't reach their ends.
Inputs may be any that keep to these rules, and one draw needn't show every extreme that they name: `expert_ids`: each row names 8 different experts; among the rows of one device no expert is named more than 4 times. `lengths`: cache positions at and beyond a request's length hold no keys for it.
All inputs are finite; a program needn't handle non-finite values.
Results may differ from the reference program's by a relative error of at most 0.0054.
Values may be sent and summed in bfloat16 or wider, within the bound.
No kernel may reach another device: no remote copies, remote signals or barrier semaphores. Data moves between devices by JAX's collectives and lax.ppermute only.
A program may use at most 128 MiB of HBM per device.

```python
import math
import jax
import jax.numpy as jnp
import numpy as np
from jax import lax

D = 4096
HEADS = 32
KV_HEADS = 4
HEAD_DIM = 128
FF_E = 512
TOP = 8
BLOCK = 32
TOK_DEV = 8
REQUESTS = 8
TOKENS = 256
LEN = 4096
EXPERTS = 32
CAP = 4
N_GROUP = 4
N_CTX = 8


def draw_queries(key, part):
    drawn = jnp.clip(jax.random.normal(jax.random.fold_in(key, 11), (TOKENS, HEADS * HEAD_DIM), jnp.float32), -4.0, 4.0)
    return drawn.astype(jnp.bfloat16)


def draw_cache(key, part):
    drawn = jnp.clip(jax.random.normal(jax.random.fold_in(key, 12), (REQUESTS, 2, LEN, KV_HEADS * HEAD_DIM), jnp.float32), -4.0, 4.0)
    return drawn.astype(jnp.bfloat16)


def with_ends(result, rng, smallest, largest):
    place = [jax.random.randint(jax.random.fold_in(rng, axis), (), 0, length) for axis, length in enumerate(result.shape)]
    main_axis = result.shape.index(max(result.shape))
    neighbour = place[:main_axis] + [(place[main_axis] + 1) % result.shape[main_axis]] + place[main_axis + 1:]
    return result.at[tuple(place)].set(smallest).at[tuple(neighbour)].set(largest)


def block_scale(key, shape, cuts, smallest, high):
    gain = 1.0
    for dim, shards_of in cuts:
        steps = jax.random.uniform(jax.random.fold_in(jax.random.fold_in(key, 6), dim), (shards_of,), jnp.float32, smallest / len(cuts), high / len(cuts))
        gain = gain * jnp.repeat(jnp.exp(steps), shape[dim] // shards_of).reshape((-1,) + (1,) * (len(shape) - 1 - dim))
    return gain


def shared_out(stream_key, own, number, rows, count, top, most, slope):
    order = jax.random.permutation(stream_key, count)
    heavy_load, common = shares(count, rows * top, most, slope, True), shares(count, rows * top, most, slope, False)
    places = jnp.arange(count)

    def named(sizes, offset_by):
        used = int((sizes > 0).sum())
        fixed = max(1, used // 4)
        moved = fixed + (places - fixed + offset_by * (used - fixed)) % max(1, count - fixed)
        return jnp.zeros((count,), jnp.int32).at[order[jnp.where(places < fixed, places, moved)]].set(jnp.asarray(sizes, jnp.int32))

    sizes = jnp.where(number % 4 == 0, named(heavy_load, number // 4), named(common, number - number // 4 - 1))
    mixed = jax.random.permutation(jax.random.fold_in(own, 3), count)
    donor, receiver = mixed[0:count // 2 * 2:2], mixed[1:count // 2 * 2:2]
    margin = jnp.minimum(sizes[donor] - 1, most - sizes[receiver]) // 2
    margin = jnp.where((donor == order[0]) | (receiver == order[0]) | (sizes[receiver] == 0), 0, jnp.maximum(margin, 0))
    moved = jax.random.randint(jax.random.fold_in(own, 4), (count // 2,), 0, 1 << 20) % (margin + 1)
    sizes = sizes.at[donor].add(-moved).at[receiver].add(moved)
    members = jnp.searchsorted(jnp.cumsum(sizes), jnp.arange(rows * top), side="right").astype(jnp.int32)
    grid = members.reshape(top, rows).T
    grid = grid[jax.random.permutation(jax.random.fold_in(own, 1), rows)]
    offset_by = jax.random.randint(jax.random.fold_in(own, 2), (rows, 1), 0, top)
    return jnp.take_along_axis(grid, (jnp.arange(top)[None, :] + offset_by) % top, axis=1)


def shares(count, total, most, skew, full):
    portions = [(1 << 20) // math.isqrt(standing ** skew) + 1 for standing in range(1, count + 1)]
    largest = most if full else min(most, max(-(-total // count), total * portions[0] // sum(portions)))
    least = 1 if total - largest >= count - 1 else 0
    given, surplus = [largest] + [least] * (count - 1), total - largest - least * (count - 1)
    while surplus > 0:
        candidates = [i for i in range(1, count) if given[i] < largest] or [i for i in range(1, count) if given[i] < most]
        mass, left = sum([portions[i] for i in candidates]), surplus
        for i in candidates:
            more = min(most - given[i], max(1, left * portions[i] // mass), surplus)
            given[i] = given[i] + more
            surplus = surplus - more
    return np.array(given)


def noise(rng, extent, spread, most, cuts=(), kind=jnp.bfloat16):
    values = spread * jax.random.normal(rng, extent, jnp.float32)
    if cuts:
        values = values * block_scale(rng, extent, cuts, -0.22, 0.18)
    return jnp.clip(values, -most, most).astype(kind)


def setup_inputs(seed: int = 0) -> dict:
    seeds = jax.random.split(jax.random.key(seed), 13)
    hidden_in = noise(seeds[0], (TOKENS, D), 0.5, 3.0, ((0, 32),))
    queries = draw_queries(jax.random.fold_in(seeds[12], 71), 0)
    block_kv = noise(seeds[2], (TOKENS, 2, KV_HEADS * HEAD_DIM), 1.0, 4.0, ((0, 32),))
    cache = draw_cache(jax.random.fold_in(seeds[12], 71), 0)
    lengths = with_ends(jax.random.randint(seeds[4], (REQUESTS,), 2, LEN + 1), jax.random.fold_in(seeds[4], 1), 2, LEN).astype(jnp.int32)
    out_proj = noise(seeds[5], (HEADS * HEAD_DIM, D), 0.25, 1.5, ((0, 8),))
    norm_gain = jnp.clip(1.0 + 0.18 * jax.random.normal(seeds[6], (D,), jnp.float32), 0.1, 1.9)
    expert_ids_keys = jax.random.split(jax.random.fold_in(seeds[7], 1), TOKENS // TOK_DEV)
    expert_ids_turns = jax.random.permutation(jax.random.fold_in(seeds[7], 3), TOKENS // TOK_DEV)
    expert_ids = jax.vmap(lambda own, number: shared_out(jax.random.fold_in(seeds[7], 2), own, number, TOK_DEV, EXPERTS, TOP, CAP, 2))(expert_ids_keys, expert_ids_turns).reshape((TOKENS, TOP))
    gate_weights = jnp.clip(jnp.exp(math.log(1.0) - 2.9957323 * jax.random.uniform(seeds[8], (TOKENS, TOP), jnp.float32) ** block_scale(seeds[8], (TOKENS, TOP), ((0, 32),), -0.2, 0.2)), 0.05, 1.0)
    expert_gate = noise(seeds[9], (EXPERTS, D, FF_E), D ** -0.5, 0.09375, ((0, 32),))
    expert_up = noise(seeds[10], (EXPERTS, D, FF_E), D ** -0.5, 0.09375, ((0, 32),))
    expert_down = noise(seeds[11], (EXPERTS, FF_E, D), FF_E ** -0.5, 0.25, ((0, 32),))
    return dict(hidden_in=hidden_in, queries=queries, block_kv=block_kv, cache=cache, lengths=lengths, out_proj=out_proj, norm_gain=norm_gain, expert_ids=expert_ids, gate_weights=gate_weights, expert_gate=expert_gate, expert_up=expert_up, expert_down=expert_down)


def attend_request(query_block, cache_pair, block_pair, length):
    group_size = HEADS // KV_HEADS
    query_heads = query_block.astype(jnp.float32).reshape(BLOCK, KV_HEADS, group_size, HEAD_DIM)
    cache_keys = cache_pair[0].reshape(LEN, KV_HEADS, HEAD_DIM)
    cache_values = cache_pair[1].reshape(LEN, KV_HEADS, HEAD_DIM)
    block_keys = block_pair[:, 0].reshape(BLOCK, KV_HEADS, HEAD_DIM)
    block_values = block_pair[:, 1].reshape(BLOCK, KV_HEADS, HEAD_DIM)
    all_keys = jnp.concatenate([cache_keys, block_keys], 0).astype(jnp.float32)
    all_values = jnp.concatenate([cache_values, block_values], 0).astype(jnp.float32)
    scores = jnp.einsum('bkgd,lkd->kgbl', query_heads, all_keys) * HEAD_DIM ** (-0.5)
    allowed = jnp.concatenate([jnp.arange(LEN, dtype=jnp.int32) < length, jnp.ones((BLOCK,), bool)])
    maximum = lax.optimization_barrier(jnp.max(jnp.where(allowed, scores, -jnp.inf), -1, keepdims=True))
    probs = jnp.where(allowed, jnp.exp(scores - maximum), 0.0)
    denominator = lax.optimization_barrier(jnp.sum(probs, -1))
    weights = probs.astype(jnp.bfloat16).astype(jnp.float32)
    numerator = jnp.einsum('kgbl,lkd->kgbd', weights, all_values)
    combined = (numerator / denominator[..., None]).astype(jnp.bfloat16)
    return combined.transpose(2, 0, 1, 3).reshape(BLOCK, HEADS * HEAD_DIM)

def reference(hidden_in, queries, block_kv, cache, lengths, out_proj, norm_gain, expert_ids, gate_weights, expert_gate, expert_up, expert_down):
    query_rows = queries.reshape(REQUESTS, BLOCK, HEADS * HEAD_DIM)
    block_rows = block_kv.reshape(REQUESTS, BLOCK, 2, KV_HEADS * HEAD_DIM)
    head_outputs = lax.map(lambda packed: attend_request(packed[0], packed[1], packed[2], packed[3]), (query_rows, cache, block_rows, lengths))
    head_outputs = head_outputs.reshape(TOKENS, HEADS * HEAD_DIM)
    attention = jnp.dot(head_outputs, out_proj, preferred_element_type=jnp.float32)
    residual = hidden_in.astype(jnp.float32) + attention
    attended = residual.astype(jnp.bfloat16)
    mean_square = lax.optimization_barrier(jnp.mean(residual * residual, -1, keepdims=True))
    normed = (residual * lax.rsqrt(mean_square + 1e-06) * norm_gain).astype(jnp.bfloat16)
    mixing = gate_weights / lax.optimization_barrier(jnp.sum(gate_weights, -1, keepdims=True))
    flat_ids = expert_ids.reshape(-1)
    flat_mixing = mixing.reshape(-1)
    most = N_GROUP * N_CTX * CAP

    def expert_step(running, inputs):
        expert, w_gate, w_up, w_down = inputs
        chosen = flat_ids == expert
        picks = jnp.nonzero(chosen, size=most, fill_value=0)[0].astype(jnp.int32)
        usable = jnp.arange(most, dtype=jnp.int32) < jnp.sum(chosen.astype(jnp.int32))
        token_at = picks // TOP
        rows = normed[token_at]
        gate_proj = jnp.dot(rows, w_gate, preferred_element_type=jnp.float32)
        up_proj = jnp.dot(rows, w_up, preferred_element_type=jnp.float32)
        activated = (jax.nn.silu(gate_proj) * up_proj).astype(jnp.bfloat16)
        expert_out = jnp.dot(activated, w_down, preferred_element_type=jnp.float32).astype(jnp.bfloat16)
        factor = jnp.where(usable, flat_mixing[picks], 0.0)
        running = running.at[token_at].add(factor[:, None] * expert_out.astype(jnp.float32))
        return (running, None)
    start_sum = jnp.zeros((TOKENS, D), jnp.float32)
    expert_sum, _ = lax.scan(expert_step, start_sum, (jnp.arange(EXPERTS, dtype=jnp.int32), expert_gate, expert_up, expert_down))
    layer_out = (residual + expert_sum).astype(jnp.bfloat16)
    return (attended, layer_out)
```

```python
import functools

import jax
import jax.numpy as jnp
from jax import lax
from jax.experimental import pallas as pl
from jax.experimental.pallas import tpu as pltpu
from jax.sharding import Mesh
from jax.sharding import PartitionSpec as P

HEAD_DIM = 128
BLOCK = 32
LANES = 128
FLOOR = -1e30

VMEM = pl.BlockSpec(memory_space=pltpu.VMEM)
SMEM = pl.BlockSpec(memory_space=pltpu.SMEM)
F32 = jnp.float32
BF16 = jnp.bfloat16


def call(kernel, outs, n_in, limit, smem=(), scratch=(), flops=0, moved=0, name=None):
    specs = [SMEM if i in smem else VMEM for i in range(n_in)]
    return pl.pallas_call(
        kernel,
        out_shape=outs,
        in_specs=specs,
        out_specs=jax.tree.map(lambda _: VMEM, outs),
        scratch_shapes=list(scratch),
        compiler_params=pltpu.CompilerParams(vmem_limit_bytes=limit << 20),
        cost_estimate=pl.CostEstimate(flops=flops, bytes_accessed=moved, transcendentals=0),
        name=name,
    )


def shape(dims, dtype):
    return jax.ShapeDtypeStruct(tuple(dims), dtype)


def attend(geo, *refs):
    nz, tok, hd, group_size, chips_per_request = geo
    slots = 2 * nz
    q_refs = refs[:slots]
    cache_ref, block_ref, len_ref, keep_ref, send_ref, kb_ref, vb_ref = refs[slots:]
    z, core = lax.axis_index("z"), lax.axis_index("core")
    cache_dev = cache_ref.shape[2]
    scale = HEAD_DIM ** (-0.5)
    first = (2 * z + core) * cache_dev
    kb_ref[...] = jnp.zeros_like(kb_ref)
    vb_ref[...] = jnp.zeros_like(vb_ref)
    kb_ref[0:tok, :] = block_ref[:, 0, :].astype(F32)
    vb_ref[0:tok, :] = block_ref[:, 1, :].astype(F32)
    span = 2 * chips_per_request * tok
    piece = chips_per_request * tok
    rows = 2 * hd * span
    column = lax.broadcasted_iota(jnp.int32, (rows, cache_dev), 1)
    block_valid = lax.broadcasted_iota(jnp.int32, (rows, LANES), 1) < tok
    lane = lax.broadcasted_iota(jnp.int32, (span, LANES), 1)

    def chip(k, carry):
        there = jnp.bitwise_xor(z, k)
        kv = pl.multiple_of(lax.div(there * (2 * hd), group_size) * HEAD_DIM, HEAD_DIM)
        for rr in range(nz // chips_per_request):
            request = jnp.bitwise_xor(lax.div(z, chips_per_request), rr)
            parts = []
            for half in range(2):
                for h in range(hd):
                    head = (2 * there + jnp.bitwise_xor(core, half)) * hd + h
                    at = pl.multiple_of(head * HEAD_DIM, HEAD_DIM)
                    for dc in range(2):
                        for kk in range(chips_per_request):
                            slot = q_refs[dc * nz + rr * chips_per_request + kk]
                            parts.append(slot[:, pl.ds(at, HEAD_DIM)].astype(F32))
            query = jnp.concatenate(parts, 0).astype(BF16)
            keys = cache_ref[request, 0, :, pl.ds(kv, HEAD_DIM)]
            values = cache_ref[request, 1, :, pl.ds(kv, HEAD_DIM)]
            contract = (((1,), (1,)), ((), ()))
            scores = lax.dot_general(query, keys, contract, preferred_element_type=F32) * scale
            allowed = column < len_ref[request] - first
            scores = jnp.where(allowed, scores, FLOOR)
            peak = jnp.max(scores, -1, keepdims=True)
            if rr == 0:
                block_keys = kb_ref[:, pl.ds(kv, HEAD_DIM)].astype(BF16)
                block_scores = (
                    lax.dot_general(query, block_keys, contract, preferred_element_type=F32) * scale
                )
                block_scores = jnp.where(block_valid, block_scores, FLOOR)
                peak = jnp.maximum(peak, jnp.max(block_scores, -1, keepdims=True))
            peak = peak.astype(BF16).astype(F32)
            probs = jnp.where(allowed, jnp.exp(scores - peak), 0.0)
            total = jnp.sum(probs, -1, keepdims=True)
            summed = jnp.dot(probs.astype(BF16), values, preferred_element_type=F32)
            if rr == 0:
                block_probs = jnp.where(block_valid, jnp.exp(block_scores - peak), 0.0)
                total = total + jnp.sum(block_probs, -1, keepdims=True)
                block_values = vb_ref[:, pl.ds(kv, HEAD_DIM)].astype(BF16)
                summed = summed + jnp.dot(
                    block_probs.astype(BF16), block_values, preferred_element_type=F32
                )
            total_high = total.astype(BF16).astype(F32)
            total_low = total - total_high
            for half, out_ref in ((0, keep_ref), (1, send_ref)):
                stats = jnp.zeros((span, LANES), F32)
                for h in range(hd):
                    at = (half * hd + h) * span
                    chunk = summed[at : at + span].astype(BF16)
                    for dc in range(2):
                        to = dc * nz * tok + rr * piece
                        out_ref[k, to : to + piece, h * HEAD_DIM : (h + 1) * HEAD_DIM] = chunk[
                            dc * piece : (dc + 1) * piece
                        ]
                    stats = jnp.where(lane == h, peak[at : at + span], stats)
                    stats = jnp.where(lane == hd + h, total_high[at : at + span], stats)
                    stats = jnp.where(lane == 2 * hd + h, total_low[at : at + span], stats)
                stats = stats.astype(BF16)
                for dc in range(2):
                    to = dc * nz * tok + rr * piece
                    out_ref[k, to : to + piece, hd * HEAD_DIM :] = stats[
                        dc * piece : (dc + 1) * piece
                    ]
        return carry

    lax.fori_loop(0, nz, chip, 0, unroll=nz <= 4)


def realigned(view, flip, k, nz, tok):
    view = view.astype(F32)
    order = [((dc ^ flip) * nz + (kk ^ k)) * tok for dc in range(2) for kk in range(nz)]
    return jnp.concatenate([view[at : at + tok] for at in order], 0)


def merged(views, hd):
    stats = [v[:, hd * HEAD_DIM :] for v in views]
    numerators, totals, peaks = [], [], []
    for h in range(hd):
        peak = [s[:, h : h + 1] for s in stats]
        total = [s[:, hd + h : hd + h + 1] + s[:, 2 * hd + h : 2 * hd + h + 1] for s in stats]
        top = functools.reduce(jnp.maximum, peak)
        factor = [jnp.exp(p - top) for p in peak]
        cut = slice(h * HEAD_DIM, (h + 1) * HEAD_DIM)
        numerators.append(sum(f * v[:, cut] for f, v in zip(factor, views)))
        totals.append(sum(f * t for f, t in zip(factor, total)))
        peaks.append(top)
    return numerators, totals, peaks


def merge_pair(hd, nz, tok, keep_ref, got_ref, *out_refs):
    rows = keep_ref.shape[1]
    lane = lax.broadcasted_iota(jnp.int32, (rows, LANES), 1)
    for k in range(nz):
        numerators, totals, peaks = merged(
            [keep_ref[k].astype(F32), realigned(got_ref[k], 1, 0, nz, tok)], hd
        )
        stats = jnp.zeros((rows, LANES), F32)
        for h in range(hd):
            high = totals[h].astype(BF16).astype(F32)
            stats = jnp.where(lane == h, peaks[h], stats)
            stats = jnp.where(lane == hd + h, high, stats)
            stats = jnp.where(lane == 2 * hd + h, totals[h] - high, stats)
            out_refs[k][:, h * HEAD_DIM : (h + 1) * HEAD_DIM] = numerators[h].astype(BF16)
        out_refs[k][:, hd * HEAD_DIM :] = stats.astype(BF16)


def project(hd, nz, tok, *refs):
    slots, (w_ref, keep_ref, send_ref) = refs[:nz], refs[nz:]
    numerators, totals, _ = merged([realigned(s[...], 0, k, nz, tok) for k, s in enumerate(slots)], hd)
    heads = jnp.concatenate([n / t for n, t in zip(numerators, totals)], 1)
    high = heads.astype(BF16)
    low = (heads - high.astype(F32)).astype(BF16)
    rows = heads.shape[0]
    half = rows // 2
    heads = jnp.concatenate([high, low], 0)
    width = w_ref.shape[1]
    step = min(width, 1024)
    for at in range(0, width, step):
        out = jnp.dot(heads, w_ref[:, at : at + step], preferred_element_type=F32)
        out = out[:rows] + out[rows:]
        keep_ref[:, at : at + step] = out[:half]
        send_ref[:, at : at + step] = out[half:]


def add_pair(nz, tok, keep_ref, got_ref, own_ref, *out_refs):
    total = keep_ref[...] + got_ref[...].astype(F32)
    own_ref[...] = total[:tok]
    for k in range(1, nz):
        out_refs[k - 1][...] = total[k * tok : (k + 1) * tok].astype(BF16)


def normalize(nz, experts, *refs):
    hidden_ref, own_ref = refs[:2]
    got = refs[2 : nz + 1]
    gain_ref, ids_ref, gates_ref, attended_ref, residual_ref, out_ref = refs[nz + 1 :]
    attention = own_ref[...]
    for ref in got:
        attention = attention + ref[...].astype(F32)
    residual = hidden_ref[...].astype(F32) + attention
    residual_ref[...] = residual
    attended_ref[...] = residual.astype(BF16)
    mean_square = jnp.mean(residual * residual, -1, keepdims=True)
    normed = residual * lax.rsqrt(mean_square + 1e-06) * gain_ref[...]
    width = residual.shape[1]
    out_ref[:, :width] = normed.astype(BF16)
    gates = gates_ref[...]
    mixing = gates / jnp.sum(gates, -1, keepdims=True)
    high = mixing.astype(BF16).astype(F32)
    low = mixing - high
    ids = ids_ref[...]
    extra = out_ref.shape[1] - width
    lane = lax.broadcasted_iota(jnp.int32, (residual.shape[0], extra), 1)
    mix = jnp.zeros((residual.shape[0], extra), F32)
    for k in range(ids.shape[1]):
        expert = ids[:, k : k + 1]
        mix = jnp.where(lane == expert, high[:, k : k + 1], mix)
        mix = jnp.where(lane == expert + experts, low[:, k : k + 1], mix)
    out_ref[:, width:] = mix.astype(BF16)


def expert(n_sets, experts, *refs):
    sets = refs[: 2 * n_sets]
    gate_ref, up_ref, down_ref = refs[2 * n_sets : 2 * n_sets + 3]
    keeps = refs[2 * n_sets + 3 : 3 * n_sets + 3]
    sends = refs[3 * n_sets + 3 : 4 * n_sets + 3]
    mine = (lax.axis_index("group") * lax.axis_size("z") + lax.axis_index("z")) * 2 + lax.axis_index("core")
    rows = sets[0].shape[0]
    width = gate_ref.shape[1]
    per = max(1, 256 // rows)
    for start in range(0, 2 * n_sets, per):
        held = [s[...] for s in sets[start : start + per]]
        x = jnp.concatenate([h[:, :width] for h in held], 0)
        mix = jnp.concatenate([h[:, width:] for h in held], 0).astype(F32)
        lane = lax.broadcasted_iota(jnp.int32, mix.shape, 1)
        chosen = (lane == mine) | (lane == mine + experts)
        mix = jnp.sum(jnp.where(chosen, mix, 0.0), -1, keepdims=True)
        gate = jnp.dot(x, gate_ref[0], preferred_element_type=F32)
        up = jnp.dot(x, up_ref[0], preferred_element_type=F32)
        activated = (gate / (1.0 + jnp.exp(-gate)) * up).astype(BF16)
        step = min(width, 1024)
        for at in range(0, width, step):
            out = jnp.dot(activated, down_ref[0, :, at : at + step], preferred_element_type=F32)
            out = out.astype(BF16).astype(F32) * mix
            out = out.astype(BF16)
            for i in range(len(held)):
                s = start + i
                ref = keeps[s] if s < n_sets else sends[s - n_sets]
                ref[:, at : at + step] = out[i * rows : (i + 1) * rows]


def add_all(n, split, *refs):
    total = refs[0][...].astype(F32)
    for ref in refs[1:n]:
        total = total + ref[...].astype(F32)
    outs = refs[n:]
    if split is None:
        outs[0][...] = total.astype(outs[0].dtype)
        return
    for k, out in enumerate(outs):
        out[...] = total[k * split : (k + 1) * split].astype(out.dtype)


def swap(x, axis, k, n):
    return lax.ppermute(x, axis, [(i, i ^ k) for i in range(n)])


def body(hidden_in, queries, block_kv, cache, lengths, out_proj, norm_gain, expert_ids, gate_weights, expert_gate, expert_up, expert_down):
    nz, ng = lax.axis_size("z"), lax.axis_size("group")
    tok, width = hidden_in.shape
    requests, _, cache_dev, kv_width = cache.shape
    num_heads = queries.shape[1] // HEAD_DIM
    group_size = num_heads * HEAD_DIM // kv_width
    hd = num_heads // (2 * nz)
    cpr = BLOCK // (2 * tok)
    experts = expert_gate.shape[0] * ng * nz * 2
    tokens = 2 * nz * tok
    block_kv = block_kv

    mine = [queries] + [swap(queries, "z", k, nz) for k in range(1, nz)]
    other = [swap(q, "core", 1, 2) for q in mine]
    slot = hd * HEAD_DIM + LANES
    part = shape((nz, tokens, slot), BF16)
    keep, send = call(
        functools.partial(attend, (nz, tok, hd, group_size, cpr)),
        (part, part),
        2 * nz + 3,
        24,
        smem=(2 * nz + 2,),
        scratch=[pltpu.VMEM((LANES, kv_width), F32)] * 2,
        flops=4 * tokens * num_heads * HEAD_DIM * cache_dev,
        moved=cache.size * 2,
        name="attend",
    )(*mine, *other, cache, block_kv, lengths)
    got = swap(send, "core", 1, 2)
    pairs = call(
        functools.partial(merge_pair, hd, nz, tok),
        [shape((tokens, slot), BF16)] * nz,
        2,
        12,
        name="merge_pair",
    )(keep, got)
    slots = [pairs[0]] + [swap(pairs[k], "z", k, nz) for k in range(1, nz)]
    keep, send = call(
        functools.partial(project, hd, nz, tok),
        (shape((tokens // 2, width), F32), shape((tokens // 2, width), F32)),
        nz + 1,
        16,
        flops=2 * tokens * out_proj.size,
        moved=out_proj.size * 2,
        name="project",
    )(*slots, out_proj)
    got = swap(send, "core", 1, 2)
    own, *away = call(
        functools.partial(add_pair, nz, tok),
        [shape((tok, width), F32)] + [shape((tok, width), BF16)] * (nz - 1),
        2,
        12,
        name="add_pair",
    )(keep, got)
    got = [swap(away[k - 1], "z", k, nz) for k in range(1, nz)]
    extra = -(-2 * experts // LANES) * LANES
    attended, residual, normed = call(
        functools.partial(normalize, nz, experts),
        (shape((tok, width), BF16), shape((tok, width), F32), shape((tok, width + extra), BF16)),
        nz + 4,
        8,
        name="normalize",
    )(hidden_in, own, *got, norm_gain.reshape(1, width), expert_ids, gate_weights)
    column = [normed] + [swap(normed, "z", k, nz) for k in range(1, nz)]
    column = jnp.concatenate(column, 0)
    near = [column] + [swap(column, "group", g, ng) for g in range(1, ng)]
    far = [swap(c, "core", 1, 2) for c in near]
    rows = nz * tok
    outs = call(
        functools.partial(expert, ng, experts),
        [shape((rows, width), BF16)] * (2 * ng),
        2 * ng + 3,
        40,
        flops=6 * 2 * ng * rows * expert_gate.size,
        moved=expert_gate.size * 6,
        name="expert",
    )(*near, *far, expert_gate, expert_up, expert_down)
    keeps, sends = outs[:ng], outs[ng:]
    gots = [swap(s, "core", 1, 2) for s in sends]
    sums = [
        call(
            functools.partial(add_all, 2, None),
            [shape((rows, width), F32 if g == 0 else BF16)],
            2,
            8,
            name="add_core",
        )(keeps[g], gots[g])[0]
        for g in range(ng)
    ]
    back = [sums[0]] + [swap(sums[g], "group", g, ng) for g in range(1, ng)]
    own, *away = call(
        functools.partial(add_all, ng, tok),
        [shape((tok, width), F32)] + [shape((tok, width), BF16)] * (nz - 1),
        ng,
        12,
        name="add_group",
    )(*back)
    got = [swap(away[k - 1], "z", k, nz) for k in range(1, nz)]
    layer_out = call(
        functools.partial(add_all, nz + 1, None),
        [shape((tok, width), BF16)],
        nz + 1,
        8,
        name="finish",
    )(residual, own, *got)[0]
    return attended, layer_out


def solution(mesh):
    groups, ctx = mesh.devices.shape
    split = Mesh(mesh.devices.reshape(groups, ctx // 2, 2), ("group", "z", "core"))
    every, across = ("group", "z", "core"), ("z", "core")
    in_specs = (
        P(every, None),
        P(every, None),
        P(every, None, None),
        P("group", None, across, None),
        P("group"),
        P(across, None),
        P(),
        P(every, None),
        P(every, None),
        P(every, None, None),
        P(every, None, None),
        P(every, None, None),
    )
    out_specs = (P(every, None), P(every, None))
    return jax.shard_map(body, mesh=split, in_specs=in_specs, out_specs=out_specs, check_vma=False)
```

```python
import functools

import jax
import jax.numpy as jnp
from jax import lax
from jax.experimental import pallas as pl
from jax.experimental.pallas import tpu as pltpu
from jax.sharding import Mesh
from jax.sharding import PartitionSpec as P

HEAD_DIM = 128
BLOCK = 32
LANES = 128
FLOOR = -1e30
EXPERT_MIB = 16

VMEM = pl.BlockSpec(memory_space=pltpu.VMEM)
SMEM = pl.BlockSpec(memory_space=pltpu.SMEM)
F32 = jnp.float32
BF16 = jnp.bfloat16


def call(kernel, outs, n_in, limit, smem=(), scratch=(), flops=0, moved=0):
    specs = [SMEM if i in smem else VMEM for i in range(n_in)]
    return pl.pallas_call(
        kernel,
        out_shape=outs,
        in_specs=specs,
        out_specs=jax.tree.map(lambda _: VMEM, outs),
        scratch_shapes=list(scratch),
        compiler_params=pltpu.CompilerParams(vmem_limit_bytes=limit << 20),
        cost_estimate=pl.CostEstimate(flops=flops, bytes_accessed=moved, transcendentals=0),
    )


def shape(dims, dtype):
    return jax.ShapeDtypeStruct(tuple(dims), dtype)


def attend(geo, *refs):
    nz, tok, heads, group_size, chips_per_request, stacked = geo
    q_refs = refs[:nz]
    own_ref, other_ref, own_block_ref, other_block_ref, len_ref = refs[nz : nz + 5]
    out_refs, (kb_ref, vb_ref) = refs[nz + 5 : -2], refs[-2:]
    z, core = lax.axis_index("z"), lax.axis_index("core")
    cache_dev = own_ref.shape[2]
    scale = HEAD_DIM ** (-0.5)
    kb_ref[...] = jnp.zeros_like(kb_ref)
    vb_ref[...] = jnp.zeros_like(vb_ref)
    for i, ref in enumerate((own_block_ref, other_block_ref)):
        kb_ref[i * tok : (i + 1) * tok, :] = ref[:, 0, :].astype(F32)
        vb_ref[i * tok : (i + 1) * tok, :] = ref[:, 1, :].astype(F32)
    span = chips_per_request * tok
    rows = heads * span
    column = lax.broadcasted_iota(jnp.int32, (rows, cache_dev), 1)
    block_valid = lax.broadcasted_iota(jnp.int32, (rows, LANES), 1) < 2 * tok
    lane = lax.broadcasted_iota(jnp.int32, (span, LANES), 1)
    contract = (((1,), (1,)), ((), ()))

    def chip(k, carry):
        there = jnp.bitwise_xor(z, k)
        kv = pl.multiple_of(lax.div(there * heads, group_size) * HEAD_DIM, HEAD_DIM)
        for rr in range(nz // chips_per_request):
            request = jnp.bitwise_xor(lax.div(z, chips_per_request), rr)
            parts = []
            for h in range(heads):
                at = pl.multiple_of((there * heads + h) * HEAD_DIM, HEAD_DIM)
                for kk in range(chips_per_request):
                    slot = q_refs[rr * chips_per_request + kk]
                    parts.append(slot[:, pl.ds(at, HEAD_DIM)].astype(F32))
            query = jnp.concatenate(parts, 0).astype(BF16)
            length = len_ref[request, 0:1, 0:1]
            scores, allowed, values = [], [], []
            for ref, c in ((own_ref, core), (other_ref, 1 - core)):
                keys = ref[request, 0, :, pl.ds(kv, HEAD_DIM)]
                valid = column < length - (2 * z + c) * cache_dev
                score = lax.dot_general(query, keys, contract, preferred_element_type=F32) * scale
                scores.append(jnp.where(valid, score, FLOOR))
                allowed.append(valid)
                values.append(ref[request, 1, :, pl.ds(kv, HEAD_DIM)])
            if rr == 0:
                keys = kb_ref[:, pl.ds(kv, HEAD_DIM)].astype(BF16)
                score = lax.dot_general(query, keys, contract, preferred_element_type=F32) * scale
                scores.append(jnp.where(block_valid, score, FLOOR))
                allowed.append(block_valid)
                values.append(vb_ref[:, pl.ds(kv, HEAD_DIM)].astype(BF16))
            peak = jnp.maximum(jnp.max(scores[0], -1, keepdims=True), jnp.max(scores[1], -1, keepdims=True))
            if rr == 0:
                peak = jnp.maximum(peak, jnp.max(scores[2], -1, keepdims=True))
            peak = peak.astype(BF16).astype(F32)
            total, summed = 0.0, 0.0
            for score, valid, value in zip(scores, allowed, values):
                probs = jnp.where(valid, jnp.exp(score - peak), 0.0)
                total = total + jnp.sum(probs, -1, keepdims=True)
                summed = summed + jnp.dot(probs.astype(BF16), value, preferred_element_type=F32)
            total_high = total.astype(BF16).astype(F32)
            total_low = total - total_high
            stats = jnp.zeros((span, LANES), F32)
            to = slice(rr * span, (rr + 1) * span)
            for h in range(heads):
                at = slice(h * span, (h + 1) * span)
                cut = slice(h * HEAD_DIM, (h + 1) * HEAD_DIM)
                if stacked:
                    out_refs[0][k, to, cut] = summed[at].astype(BF16)
                else:
                    out_refs[k][to, cut] = summed[at].astype(BF16)
                stats = jnp.where(lane == h, peak[at], stats)
                stats = jnp.where(lane == heads + h, total_high[at], stats)
                stats = jnp.where(lane == 2 * heads + h, total_low[at], stats)
            if stacked:
                out_refs[0][k, to, heads * HEAD_DIM :] = stats.astype(BF16)
            else:
                out_refs[k][to, heads * HEAD_DIM :] = stats.astype(BF16)
        return carry

    if stacked:
        lax.fori_loop(0, nz, chip, 0)
    else:
        for k in range(nz):
            chip(k, 0)


def realigned(view, k, nz, tok):
    view = view.astype(F32)
    return jnp.concatenate([view[(i ^ k) * tok : ((i ^ k) + 1) * tok] for i in range(nz)], 0)


def project(heads, nz, tok, *refs):
    slots, (own_ref, other_ref), out_refs = refs[:nz], refs[nz : nz + 2], refs[nz + 2 :]
    views = [realigned(s[...], k, nz, tok) for k, s in enumerate(slots)]
    stats = [v[:, heads * HEAD_DIM :] for v in views]
    outputs = []
    for h in range(heads):
        peak = [s[:, h : h + 1] for s in stats]
        total = [s[:, heads + h : heads + h + 1] + s[:, 2 * heads + h : 2 * heads + h + 1] for s in stats]
        top = functools.reduce(jnp.maximum, peak)
        factor = [jnp.exp(p - top) for p in peak]
        cut = slice(h * HEAD_DIM, (h + 1) * HEAD_DIM)
        numerator = sum(f * v[:, cut] for f, v in zip(factor, views))
        outputs.append(numerator / sum(f * t for f, t in zip(factor, total)))
    mixed = jnp.concatenate(outputs, 1)
    high = mixed.astype(BF16)
    low = (mixed - high.astype(F32)).astype(BF16)
    rows = mixed.shape[0]
    both = jnp.concatenate([high, low], 0)
    half = both.shape[1] // 2
    first = lax.axis_index("core") == 0
    left, right = both[:, :half], both[:, half:]
    mine, theirs = jnp.where(first, left, right), jnp.where(first, right, left)
    width = own_ref.shape[1]
    step = min(width, 1024)
    for at in range(0, width, step):
        cut = slice(at, at + step)
        out = jnp.dot(mine, own_ref[:, cut], preferred_element_type=F32)
        out = out + jnp.dot(theirs, other_ref[:, cut], preferred_element_type=F32)
        out = out[:rows] + out[rows:]
        for k, ref in enumerate(out_refs):
            ref[:, cut] = out[k * tok : (k + 1) * tok].astype(ref.dtype)


def normalize(nz, experts, *refs):
    hidden_ref, own_ref = refs[:2]
    got = refs[2 : nz + 1]
    gain_ref, ids_ref, gates_ref, attended_ref, residual_ref, out_ref = refs[nz + 1 :]
    attention = own_ref[...]
    for ref in got:
        attention = attention + ref[...].astype(F32)
    residual = hidden_ref[...].astype(F32) + attention
    residual_ref[...] = residual
    attended_ref[...] = residual.astype(BF16)
    mean_square = jnp.mean(residual * residual, -1, keepdims=True)
    normed = residual * lax.rsqrt(mean_square + 1e-06) * gain_ref[...]
    width = residual.shape[1]
    out_ref[:, :width] = normed.astype(BF16)
    gates = gates_ref[...]
    mixing = gates / jnp.sum(gates, -1, keepdims=True)
    high = mixing.astype(BF16).astype(F32)
    low = mixing - high
    ids = ids_ref[...]
    extra = out_ref.shape[1] - width
    lane = lax.broadcasted_iota(jnp.int32, (residual.shape[0], extra), 1)
    mix = jnp.zeros((residual.shape[0], extra), F32)
    for k in range(ids.shape[1]):
        expert = ids[:, k : k + 1]
        mix = jnp.where(lane == expert, high[:, k : k + 1], mix)
        mix = jnp.where(lane == expert + experts, low[:, k : k + 1], mix)
    out_ref[:, width:] = mix.astype(BF16)


def expert(ng, experts, *refs):
    inputs, weights = refs[: 2 * ng], refs[2 * ng : 2 * ng + 6]
    out_refs, (x_ref, act_ref) = refs[2 * ng + 6 : -2], refs[-2:]
    width = x_ref.shape[1]
    mine = (lax.axis_index("group") * lax.axis_size("z") + lax.axis_index("z")) * 2 + lax.axis_index("core")
    extra = []
    at = 0
    for ref in inputs:
        x_ref[at : at + ref.shape[0], :] = ref[:, :width]
        extra.append(ref[:, width:].astype(F32))
        at += ref.shape[0]
    extra = jnp.concatenate(extra, 0)
    lane = lax.broadcasted_iota(jnp.int32, extra.shape, 1)
    mix = []
    for e in range(2):
        who = jnp.bitwise_xor(mine, e)
        chosen = (lane == who) | (lane == who + experts)
        mix.append(jnp.sum(jnp.where(chosen, extra, 0.0), -1, keepdims=True))
        gate_ref, up_ref, _ = weights[3 * e : 3 * e + 3]
        hidden = gate_ref.shape[2]
        step = min(hidden, 256)
        for at in range(0, hidden, step):
            cut = slice(at, at + step)
            x = x_ref[...]
            gate = jnp.dot(x, gate_ref[0, :, cut], preferred_element_type=F32)
            up = jnp.dot(x, up_ref[0, :, cut], preferred_element_type=F32)
            act_ref[e, :, cut] = (gate / (1.0 + jnp.exp(-gate)) * up).astype(BF16)
    step = min(width, 512)
    for at in range(0, width, step):
        cut = slice(at, at + step)
        out = 0.0
        for e in range(2):
            y = jnp.dot(act_ref[e], weights[3 * e + 2][0, :, cut], preferred_element_type=F32)
            out = out + y.astype(BF16).astype(F32) * mix[e]
        row = 0
        for ref in out_refs:
            ref[:, cut] = out[row : row + ref.shape[0]].astype(ref.dtype)
            row += ref.shape[0]


def add_all(n, split, *refs):
    total = refs[0][...].astype(F32)
    for ref in refs[1:n]:
        total = total + ref[...].astype(F32)
    outs = refs[n:]
    if split is None:
        outs[0][...] = total.astype(outs[0].dtype)
        return
    for k, out in enumerate(outs):
        out[...] = total[k * split : (k + 1) * split].astype(out.dtype)


def held(x, lengths):
    return jnp.where(lengths[0] > 0, x, jnp.zeros_like(x))


def swap(x, axis, k, n):
    return lax.ppermute(x, axis, [(i, i ^ k) for i in range(n)])


def after(x, *others):
    return lax.optimization_barrier((x, *others))[0]


def body(hidden_in, queries, block_kv, cache, lengths, out_proj, norm_gain, expert_ids, gate_weights, expert_gate, expert_up, expert_down):
    nz, ng = lax.axis_size("z"), lax.axis_size("group")
    tok, width = hidden_in.shape
    _, _, cache_dev, kv_width = cache.shape
    num_heads = queries.shape[1] // HEAD_DIM
    group_size = num_heads * HEAD_DIM // kv_width
    heads = num_heads // nz
    chips = BLOCK // (2 * tok)
    experts = expert_gate.shape[0] * ng * nz * 2
    rows = nz * tok
    away = range(1, nz)

    slots = [swap(queries, "z", k, nz) for k in away]
    other_cache = swap(cache, "core", 1, 2)
    other_block = swap(block_kv, "core", 1, 2)
    other_proj = swap(after(out_proj, *slots), "core", 1, 2)
    own_proj = held(out_proj, lengths)
    cache = held(cache, lengths)
    queries = held(queries, lengths)
    block_kv = held(block_kv, lengths)
    lengths = jnp.broadcast_to(lengths[:, None, None], (lengths.shape[0], 8, LANES))
    slots = [queries] + slots

    slot = heads * HEAD_DIM + LANES
    stacked = nz > 4
    outs = [shape((nz, rows, slot), BF16)] if stacked else [shape((rows, slot), BF16)] * nz
    parts = call(
        functools.partial(attend, (nz, tok, heads, group_size, chips, stacked)),
        outs,
        nz + 5,
        16 if nz <= 4 else 40,
        scratch=[pltpu.VMEM((LANES, kv_width), F32)] * 2,
        flops=4 * rows * num_heads * HEAD_DIM * 2 * cache_dev,
        moved=cache.size * 4,
    )(*slots, cache, other_cache, block_kv, other_block, lengths)
    if stacked:
        parts = [parts[0][k] for k in range(nz)]
    other_expert = [swap(after(w, parts[0]), "core", 1, 2) for w in (expert_gate, expert_up, expert_down)]
    slots = [parts[0]] + [swap(parts[k], "z", k, nz) for k in away]
    sums = call(
        functools.partial(project, heads, nz, tok),
        [shape((tok, width), F32)] + [shape((tok, width), BF16)] * (nz - 1),
        nz + 2,
        16,
        flops=8 * rows * out_proj.size,
        moved=out_proj.size * 4,
    )(*slots, own_proj, other_proj)
    got = [swap(sums[k], "z", k, nz) for k in away]
    extra = -(-2 * experts // LANES) * LANES
    attended, residual, normed = call(
        functools.partial(normalize, nz, experts),
        (shape((tok, width), BF16), shape((tok, width), F32), shape((tok, width + extra), BF16)),
        nz + 4,
        8,
    )(hidden_in, sums[0], *got, norm_gain.reshape(1, width), expert_ids, gate_weights)
    column = jnp.concatenate([swap(normed, "z", k, nz) for k in away], 0)
    inputs = [normed, column]
    for g in range(1, ng):
        inputs += [swap(normed, "group", g, ng), swap(column, "group", g, ng)]
    outs = []
    for g in range(ng):
        kind = F32 if g == 0 else BF16
        outs += [shape((tok, width), kind), shape((rows - tok, width), kind)]
    outs = call(
        functools.partial(expert, ng, experts),
        outs,
        2 * ng + 6,
        EXPERT_MIB if nz <= 4 else 50,
        scratch=[pltpu.VMEM((ng * rows, width), BF16), pltpu.VMEM((2, ng * rows, expert_gate.shape[2]), BF16)],
        flops=12 * ng * rows * expert_gate.size,
        moved=expert_gate.size * 12,
    )(*inputs, expert_gate, expert_up, expert_down, *other_expert)
    back = [outs[1]] + [swap(outs[2 * g + 1], "group", g, ng) for g in range(1, ng)]
    here = [outs[0]] + [swap(outs[2 * g], "group", g, ng) for g in range(1, ng)]
    sums = call(functools.partial(add_all, ng, tok), [shape((tok, width), BF16)] * (nz - 1), ng, 12)(*back)
    got = [swap(sums[k - 1], "z", k, nz) for k in away]
    layer_out = call(
        functools.partial(add_all, nz + ng, None), [shape((tok, width), BF16)], nz + ng, 8
    )(residual, *here, *got)[0]
    return attended, layer_out


def solution(mesh):
    groups, ctx = mesh.devices.shape
    split = Mesh(mesh.devices.reshape(groups, ctx // 2, 2), ("group", "z", "core"))
    every, across = ("group", "z", "core"), ("z", "core")
    in_specs = (
        P(every, None),
        P(every, None),
        P(every, None, None),
        P("group", None, across, None),
        P("group"),
        P(across, None),
        P(),
        P(every, None),
        P(every, None),
        P(every, None, None),
        P(every, None, None),
        P(every, None, None),
    )
    out_specs = (P(every, None), P(every, None))

    return jax.shard_map(body, mesh=split, in_specs=in_specs, out_specs=out_specs, check_vma=False)
```
